32 devices in a mesh: ctx: 8 (over y, x, core), ep: 4 (over z).
Axes of the slice: x: 2, y: 2, z: 4, core: 2. Of those that a mesh axis runs over, the one named last changes fastest.
Arguments:
- out_grad: bfloat16 [2048, 2048], P('ctx'), may hold values from -12 to 12
- gate_values: bfloat16 [2048, 8], P('ctx'), may hold values from 0.049804688 to 0.3984375
- expert_ids: int32 [2048, 8], P('ctx'), may hold values from 0 to 15, all different within a row; in each aligned block of 256 rows (0 to 255, 256 to 511, ...) at most 192 rows name the same one
- segment_ids: int32 [2048], P('ctx'), may hold values from 0 to 3, never falling along the last dimension, each value on 1 to 1793 neighbouring positions
- gate_pre: bfloat16 [32, 8, 192, 512], P(('ctx', 'ep')), may hold values from -6 to 6
- up_pre: bfloat16 [32, 8, 192, 512], P(('ctx', 'ep')), may hold values from -6 to 6
- w_gate: bfloat16 [32, 2048, 512], P(('ctx', 'ep')), may hold values from -0.125 to 0.125
- w_up: bfloat16 [32, 2048, 512], P(('ctx', 'ep')), may hold values from -0.125 to 0.125
- w_down: bfloat16 [32, 512, 2048], P(('ctx', 'ep')), may hold values from -0.1875 to 0.1875
- queries: bfloat16 [2048, 2048], P('ctx', 'ep'), may hold values from -0.015625 to 0.015625
- keys: bfloat16 [2048, 2048], P('ctx', 'ep'), may hold values from -0.015625 to 0.015625
- values: bfloat16 [2048, 2048], P('ctx', 'ep'), may hold values from -6 to 6
Outputs:
- query_grad: bfloat16 [2048, 2048], P('ctx', 'ep')
- key_grad: bfloat16 [2048, 2048], P('ctx', 'ep')
- value_grad: bfloat16 [2048, 2048], P('ctx', 'ep')
- down_grad: float32 [32, 512, 2048], P(('ctx', 'ep'))
The draws below stay inside these ranges and needn't reach their ends.
Inputs may be any that keep to these rules, and one draw needn't show every extreme that they name: `expert_ids`: each token names 8 different experts. Among the 256 tokens of one context shard at most 192 name the same expert, and in every draw some shard has exactly 192 tokens that name one expert. `segment_ids`: document numbers never fall along the tokens; a document has 1 to 1793 tokens and one has exactly 1793, so that no document covers more than eight context shards of 256 tokens.
All inputs are finite; a program needn't handle non-finite values.
Results may differ from the reference program's by a relative error of at most 0.008.
Values may be sent and summed in bfloat16 or wider, within the bound.
No kernel may reach another device: no remote copies, remote signals or barrier semaphores. Data moves between devices by JAX's collectives and lax.ppermute only.
A program may use at most 128 MiB of HBM per device.

```python
import math
import jax
import jax.numpy as jnp
import numpy as np
from jax import lax

D = 2048
HEADS = 16
HEAD_DIM = 128
FF = 1024
TOP = 8
TOK_DEV = 256
EXPERTS = 16
HSPLIT = 2
FFP = 512
MOST = 192
TOKENS = 2048
DOC_MOST = 1793
DOCS = 4
N_CTX = 8


def shard_levels(key, shape, cuts, smallest, high):
    loudness, own = 1.0, jax.random.fold_in(key, 6)
    for dim, blocks in cuts:
        steps = jnp.exp(jax.random.uniform(jax.random.fold_in(own, dim), (blocks,), jnp.float32, smallest / len(cuts), high / len(cuts)))
        loudness = loudness * jnp.repeat(steps, shape[dim] // blocks).reshape([-1 if axis == dim else 1 for axis in range(len(shape))])
    return loudness


def profile(number_of, total, bound, slope):
    weights = [(1 << 20) // math.isqrt(grade ** slope) + 1 for grade in range(2, number_of + 1)]
    spare, given = total - bound - (number_of - 1), [1] * (number_of - 1)
    while spare > 0:
        free = [i for i in range(number_of - 1) if given[i] < bound]
        pool, left = sum([weights[i] for i in free]), spare
        for i in free:
            extra = min(bound - given[i], max(1, left * weights[i] // pool), spare)
            given[i] = given[i] + extra
            spare = spare - extra
    return np.array([bound] + given)


def uneven(rng, amount, total, limit, slope):
    if amount == 2:
        one = jax.random.randint(rng, (), max(1, total - limit), min(limit, total - 1) + 1)
        return jnp.stack([one, total - one])
    sizes = jnp.asarray(profile(amount, total, limit, slope), jnp.int32)
    twos = (amount - 1) // 2
    donor, sink = sizes[1:1 + 2 * twos:2], sizes[2:2 + 2 * twos:2]
    room = jnp.minimum(donor - 1, limit - sink)
    moved = jax.random.randint(jax.random.fold_in(rng, 1), (twos,), 0, 1 << 20) % (room + 1)
    sizes = sizes.at[1:1 + 2 * twos:2].set(donor - moved).at[2:2 + 2 * twos:2].set(sink + moved)
    return sizes[jax.random.permutation(jax.random.fold_in(rng, 2), amount)]


def routed_block(stream_key, own, number, rows, count, top, bound, skew):
    sequence = jax.random.permutation(stream_key, count)
    packed, common = portions_of(count, rows * top, bound, skew, True), portions_of(count, rows * top, bound, skew, False)
    places = jnp.arange(count)

    def named(sizes, turn):
        used = int((sizes > 0).sum())
        fixed = max(1, used // 4)
        moved = fixed + (places - fixed + turn * (used - fixed)) % max(1, count - fixed)
        return jnp.zeros((count,), jnp.int32).at[sequence[jnp.where(places < fixed, places, moved)]].set(jnp.asarray(sizes, jnp.int32))

    sizes = jnp.where(number % 4 == 0, named(packed, number // 4), named(common, number - number // 4 - 1))
    mixed = jax.random.permutation(jax.random.fold_in(own, 3), count)
    donor, taker = mixed[0:count // 2 * 2:2], mixed[1:count // 2 * 2:2]
    room = jnp.minimum(sizes[donor] - 1, bound - sizes[taker]) // 2
    room = jnp.where((donor == sequence[0]) | (taker == sequence[0]) | (sizes[taker] == 0), 0, jnp.maximum(room, 0))
    moved = jax.random.randint(jax.random.fold_in(own, 4), (count // 2,), 0, 1 << 20) % (room + 1)
    sizes = sizes.at[donor].add(-moved).at[taker].add(moved)
    items = jnp.searchsorted(jnp.cumsum(sizes), jnp.arange(rows * top), side="right").astype(jnp.int32)
    listing = items.reshape(top, rows).T
    listing = listing[jax.random.permutation(jax.random.fold_in(own, 1), rows)]
    turn = jax.random.randint(jax.random.fold_in(own, 2), (rows, 1), 0, top)
    return jnp.take_along_axis(listing, (jnp.arange(top)[None, :] + turn) % top, axis=1)


def portions_of(number_of, total, limit, lean, full):
    loads = [(1 << 20) // math.isqrt(rank ** lean) + 1 for rank in range(1, number_of + 1)]
    largest = limit if full else min(limit, max(-(-total // number_of), total * loads[0] // sum(loads)))
    least = 1 if total - largest >= number_of - 1 else 0
    given, surplus = [largest] + [least] * (number_of - 1), total - largest - least * (number_of - 1)
    while surplus > 0:
        movable = [i for i in range(1, number_of) if given[i] < largest] or [i for i in range(1, number_of) if given[i] < limit]
        whole, budget = sum([loads[i] for i in movable]), surplus
        for i in movable:
            more = min(limit - given[i], max(1, budget * loads[i] // whole), surplus)
            given[i] = given[i] + more
            surplus = surplus - more
    return np.array(given)


def scatter_about(rng, shape, deviation, limit, cuts=(), held_as=jnp.bfloat16):
    factor_of = shard_levels(rng, shape, cuts, -0.22, 0.18) if cuts else 1.0
    values = jax.random.normal(rng, shape, jnp.float32) * deviation * factor_of
    return jnp.minimum(jnp.maximum(values, -limit), limit).astype(held_as)


def setup_inputs(seed: int = 0) -> dict:
    key_of = jax.random.split(jax.random.key(seed), 13)
    out_grad = scatter_about(key_of[0], (TOKENS, D), 2.0, 12.0, ((0, 8),))
    gate_values = jnp.clip(0.049804688 + 0.3486328 * jax.random.uniform(key_of[1], (TOKENS, TOP), jnp.float32) ** shard_levels(key_of[1], (TOKENS, TOP), ((0, 8),), -0.2, 0.2), 0.049804688, 0.3984375).astype(jnp.bfloat16)
    expert_ids_keys = jax.random.split(jax.random.fold_in(key_of[2], 1), TOKENS // TOK_DEV)
    expert_ids_turns = jax.random.permutation(jax.random.fold_in(key_of[2], 3), TOKENS // TOK_DEV)
    expert_ids = jax.vmap(lambda own, number: routed_block(jax.random.fold_in(key_of[2], 2), own, number, TOK_DEV, EXPERTS, TOP, MOST, 2))(expert_ids_keys, expert_ids_turns).reshape((TOKENS, TOP))
    segment_ids = jnp.searchsorted(jnp.cumsum(uneven(key_of[3], DOCS, TOKENS, DOC_MOST, 2)), jnp.arange(TOKENS), side="right").astype(jnp.int32)
    gate_pre = scatter_about(key_of[4], (EXPERTS * HSPLIT, N_CTX, MOST, FFP), 1.0, 6.0, ((0, 32),))
    up_pre = scatter_about(key_of[5], (EXPERTS * HSPLIT, N_CTX, MOST, FFP), 1.0, 6.0, ((0, 32),))
    w_gate = scatter_about(key_of[6], (EXPERTS * HSPLIT, D, FFP), D ** -0.5, 0.125, ((0, 32),))
    w_up = scatter_about(key_of[7], (EXPERTS * HSPLIT, D, FFP), D ** -0.5, 0.125, ((0, 32),))
    w_down = scatter_about(key_of[8], (EXPERTS * HSPLIT, FFP, D), FF ** -0.5, 0.1875, ((0, 32),))
    queries = scatter_about(key_of[9], (TOKENS, D), (4 * HEAD_DIM * TOK_DEV) ** -0.5, 0.015625, ((0, 8), (1, 4)))
    keys = scatter_about(key_of[10], (TOKENS, D), (4 * HEAD_DIM * TOK_DEV) ** -0.5, 0.015625, ((0, 8), (1, 4)))
    values = scatter_about(key_of[11], (TOKENS, D), 1.0, 6.0, ((0, 8), (1, 4)))
    return {"out_grad": out_grad, "gate_values": gate_values, "expert_ids": expert_ids, "segment_ids": segment_ids, "gate_pre": gate_pre, "up_pre": up_pre, "w_gate": w_gate, "w_up": w_up, "w_down": w_down, "queries": queries, "keys": keys, "values": values}


HIGHEST = lax.Precision.HIGHEST


def assignment_ranks(expert_ids):
    shards = expert_ids.reshape(N_CTX, TOK_DEV * TOP)
    labels = jnp.arange(EXPERTS, dtype=jnp.int32)

    def count_before(assignment_row):
        onehot = (assignment_row[:, None] == labels[None, :]).astype(jnp.int32)
        before = jnp.cumsum(onehot, axis=0) - onehot
        return jnp.sum(before * onehot, axis=1).astype(jnp.int32)

    return lax.map(count_before, shards).reshape(TOKENS * TOP)


def expert_rows(cotangent, pre_gate, pre_up, gate_matrix, up_matrix, down_matrix):
    down_part = lax.dot_general(cotangent, down_matrix, (((1,), (1,)), ((), ())), preferred_element_type=jnp.float32)
    gate_value = pre_gate.astype(jnp.float32)
    up_value = pre_up.astype(jnp.float32)
    sigmoid_gate = jax.nn.sigmoid(gate_value)
    hidden = (gate_value * sigmoid_gate * up_value).astype(jnp.bfloat16)
    down_grad = lax.dot_general(hidden, cotangent, (((0,), (0,)), ((), ())), preferred_element_type=jnp.float32)
    gate_delta = (down_part * up_value * sigmoid_gate * (1.0 + gate_value * (1.0 - sigmoid_gate))).astype(jnp.bfloat16)
    up_delta = (down_part * gate_value * sigmoid_gate).astype(jnp.bfloat16)
    input_part = lax.dot_general(gate_delta, gate_matrix, (((1,), (1,)), ((), ())), preferred_element_type=jnp.float32)
    input_part = input_part + lax.dot_general(up_delta, up_matrix, (((1,), (1,)), ((), ())), preferred_element_type=jnp.float32)
    return input_part.astype(jnp.bfloat16), down_grad


def within_block(query3, key3, value3, cot3, segment):
    positions = jnp.arange(segment.shape[0], dtype=jnp.int32)
    allowed = ((positions[:, None] >= positions[None, :]) & (segment[:, None] == segment[None, :])).astype(jnp.float32)
    query32 = query3.astype(jnp.float32)
    key32 = key3.astype(jnp.float32)
    value32 = value3.astype(jnp.float32)
    cot32 = cot3.astype(jnp.float32)
    cot_value = jnp.einsum("the,she->hts", cot32, value32, precision=HIGHEST) * allowed[None]
    query_key = jnp.einsum("the,she->hts", query32, key32, precision=HIGHEST) * allowed[None]
    query_grad = jnp.einsum("hts,she->the", cot_value, key32, precision=HIGHEST)
    key_grad = jnp.einsum("hts,the->she", cot_value, query32, precision=HIGHEST)
    value_grad = jnp.einsum("hts,the->she", query_key, cot32, precision=HIGHEST)
    return query_grad, key_grad, value_grad


def end_states(query3, key3, value3, cot3, segment):
    last_mask = (segment == segment[-1]).astype(jnp.float32)[:, None, None]
    first_mask = (segment == segment[0]).astype(jnp.float32)[:, None, None]
    forward_state = jnp.einsum("the,thf->hef", key3.astype(jnp.float32) * last_mask, value3.astype(jnp.float32), precision=HIGHEST)
    backward_state = jnp.einsum("the,thf->hef", query3.astype(jnp.float32) * first_mask, cot3.astype(jnp.float32), precision=HIGHEST)
    return forward_state, backward_state


def reference(out_grad, gate_values, expert_ids, segment_ids, gate_pre, up_pre, w_gate, w_up, w_down, queries, keys, values):
    flat_ids = expert_ids.reshape(TOKENS * TOP)
    slot_rank = assignment_ranks(expert_ids)
    token_of = (jnp.arange(TOKENS * TOP, dtype=jnp.int32) // TOP).astype(jnp.int32)
    shard_of = (token_of // TOK_DEV).astype(jnp.int32)
    flat_gates = gate_values.reshape(TOKENS * TOP)
    padded = jnp.concatenate([out_grad, jnp.zeros((1, D), out_grad.dtype)], axis=0)
    dump_slot = N_CTX * MOST

    def per_expert(y_grad, expert):
        position = jnp.where(flat_ids == expert, shard_of * MOST + slot_rank, dump_slot).astype(jnp.int32)
        slot_token = jnp.full((dump_slot,), TOKENS, jnp.int32).at[position].set(token_of, mode="drop")
        slot_gate = jnp.zeros((dump_slot,), gate_values.dtype).at[position].set(flat_gates, mode="drop")
        row_block = jnp.take(padded, slot_token, axis=0)
        cotangent = (slot_gate[:, None].astype(jnp.float32) * row_block.astype(jnp.float32)).astype(jnp.bfloat16)
        grads = []
        for hidden_part in range(HSPLIT):
            weight_row = (expert * HSPLIT + hidden_part).astype(jnp.int32)
            pre_gate = lax.dynamic_index_in_dim(gate_pre, weight_row, 0, keepdims=False).reshape(dump_slot, FFP)
            pre_up = lax.dynamic_index_in_dim(up_pre, weight_row, 0, keepdims=False).reshape(dump_slot, FFP)
            gate_matrix = lax.dynamic_index_in_dim(w_gate, weight_row, 0, keepdims=False)
            up_matrix = lax.dynamic_index_in_dim(w_up, weight_row, 0, keepdims=False)
            down_matrix = lax.dynamic_index_in_dim(w_down, weight_row, 0, keepdims=False)
            input_part, down_part_grad = expert_rows(cotangent, pre_gate, pre_up, gate_matrix, up_matrix, down_matrix)
            y_grad = y_grad.at[slot_token].add(input_part.astype(jnp.float32), mode="drop")
            grads.append(down_part_grad)
        return y_grad, jnp.stack(grads)

    y_grad, down_grads = lax.scan(per_expert, jnp.zeros((TOKENS, D), jnp.float32), jnp.arange(EXPERTS, dtype=jnp.int32))
    down_grad = down_grads.reshape(EXPERTS * HSPLIT, FFP, D)

    head_cot = y_grad.astype(jnp.bfloat16)
    block_shape = (N_CTX, TOK_DEV, HEADS, HEAD_DIM)
    seg_blocks = segment_ids.reshape(N_CTX, TOK_DEV)
    blocks = (queries.reshape(block_shape), keys.reshape(block_shape), values.reshape(block_shape), head_cot.reshape(block_shape), seg_blocks)

    def block_work(block):
        query3, key3, value3, cot3, segment = block
        inner = within_block(query3, key3, value3, cot3, segment)
        states = end_states(query3, key3, value3, cot3, segment)
        return inner + states

    inner_query, inner_key, inner_value, forward_states, backward_states = lax.map(block_work, blocks)
    firsts = seg_blocks[:, 0]
    lasts = seg_blocks[:, -1]
    empty_state = jnp.zeros((HEADS, HEAD_DIM, HEAD_DIM), jnp.float32)

    def forward_step(carried, item):
        state_sum, last_doc = carried
        local_state, first_doc, final_doc = item
        kept = jnp.where(final_doc == last_doc, state_sum, jnp.zeros_like(state_sum))
        return (local_state + kept, final_doc), (state_sum, last_doc)

    def backward_step(carried, item):
        back_sum, next_doc = carried
        local_state, first_doc, final_doc = item
        kept = jnp.where(first_doc == next_doc, back_sum, jnp.zeros_like(back_sum))
        return (local_state + kept, first_doc), (back_sum, next_doc)

    final_carry, (state_in, doc_in) = lax.scan(forward_step, (empty_state, jnp.int32(-1)), (forward_states, firsts, lasts))
    final_back, (back_in, doc_back) = lax.scan(backward_step, (empty_state, jnp.int32(-1)), (backward_states, firsts, lasts), reverse=True)

    def cross_work(block):
        key3, value3, cot3, segment, state_sum, doc_before, back_sum, doc_after = block
        before_mask = (segment == doc_before).astype(jnp.float32)[:, None, None]
        after_mask = (segment == doc_after).astype(jnp.float32)[:, None, None]
        query_part = jnp.einsum("thf,hef->the", cot3.astype(jnp.float32), state_sum, precision=HIGHEST) * before_mask
        key_part = jnp.einsum("thf,hef->the", value3.astype(jnp.float32), back_sum, precision=HIGHEST) * after_mask
        value_part = jnp.einsum("the,hef->thf", key3.astype(jnp.float32), back_sum, precision=HIGHEST) * after_mask
        return query_part, key_part, value_part

    outer_query, outer_key, outer_value = lax.map(cross_work, (blocks[1], blocks[2], blocks[3], seg_blocks, state_in, doc_in, back_in, doc_back))
    query_grad = (inner_query + outer_query).astype(jnp.bfloat16).reshape(TOKENS, D)
    key_grad = (inner_key + outer_key).astype(jnp.bfloat16).reshape(TOKENS, D)
    value_grad = (inner_value + outer_value).astype(jnp.bfloat16).reshape(TOKENS, D)
    return (query_grad, key_grad, value_grad, down_grad)
```

```python
import functools

import jax
import jax.numpy as jnp
from jax import lax
from jax.experimental import pallas as pl
from jax.experimental.pallas import tpu as pltpu
from jax.sharding import PartitionSpec as P


HEAD_DIM = 128
BF16 = jnp.bfloat16
F32 = jnp.float32


def dot(a, b, dims):
    return lax.dot_general(a, b, ((dims[:1], dims[1:]), ((), ())), preferred_element_type=F32)


def swap(x, axis, offset):
    return lax.ppermute(x, axis, [(i, i ^ offset) for i in range(lax.axis_size(axis))])


def after(x, *others):
    return lax.optimization_barrier((x, *others))[0]


def expert_kernel(scal, *refs, count, groups, tok, slots):
    routes, refs = refs[:count], refs[count:]
    early, refs = refs[:count], refs[count:]
    late, refs = refs[:count], refs[count:]
    pres, refs = refs[:count], refs[count:]
    ups, refs = refs[:count], refs[count:]
    w_down, w_gate, w_up = refs[:3]
    lows, highs = refs[3 : 3 + count], refs[3 + count : 3 + 2 * count]
    cot, hidden, token, pick, back, part, gate_delta, up_delta = refs[3 + 2 * count :]
    step = pl.program_id(0)

    @pl.when(step == 0)
    def _():
        token[...] = jnp.zeros_like(token)
        expert = scal[0].astype(F32)
        t_row = lax.broadcasted_iota(jnp.int32, (tok, tok), 0)
        t_col = lax.broadcasted_iota(jnp.int32, (tok, tok), 1)
        earlier = (t_row < t_col).astype(F32).astype(BF16)
        slot = lax.broadcasted_iota(jnp.int32, (slots, tok), 0)
        for i, route in enumerate(routes):
            gates = route[:, :tok].astype(F32)
            named = route[:, tok : 2 * tok].astype(F32) == expert
            gate = jnp.sum(jnp.where(named, gates, 0.0), axis=0, keepdims=True)
            mine = jnp.sum(named.astype(F32), axis=0, keepdims=True)
            spread = jnp.broadcast_to(mine, (8, tok)).astype(BF16)
            rank = dot(spread, earlier, (1, 0))[:1].astype(jnp.int32)
            chosen = jnp.where((slot == rank) & (mine > 0.0), 1.0, 0.0)
            pick[i] = (chosen * gate).astype(BF16)
            back[i] = chosen.T.astype(BF16)

    def gather(rows):
        for i in range(count):
            cot[i * slots : (i + 1) * slots, :] = dot(pick[i], rows[i][...], (1, 0)).astype(BF16)
        return dot(cot[...], w_down[...], (1, 1))

    @pl.when(step == 0)
    def _():
        part[...] = gather(early)

    @pl.when(step == 1)
    def _():
        part[...] += gather(late)
        for i in range(count):
            here = pl.ds(i * slots, slots)
            a = pres[i][0].astype(F32)
            u = ups[i][0].astype(F32)
            s = jax.nn.sigmoid(a)
            d = part[here, :]
            hidden[here, :] = (a * s * u).astype(BF16)
            gate_delta[here, :] = (d * u * s * (1.0 + a * (1.0 - s))).astype(BF16)
            up_delta[here, :] = (d * a * s).astype(BF16)

    @pl.when(step >= 2)
    def _():
        both = dot(gate_delta[...], w_gate[...], (1, 1)) + dot(up_delta[...], w_up[...], (1, 1))
        both = both.astype(BF16)
        half = both.shape[1] // groups
        for i in range(count):
            y = dot(back[i], both[i * slots : (i + 1) * slots], (1, 0)).astype(BF16)
            for g in range(groups // 2):
                there = pl.ds(g * half, half)
                lows[i][:, there] = y[:, 2 * g * half : (2 * g + 1) * half]
                highs[i][:, there] = y[:, (2 * g + 1) * half : (2 * g + 2) * half]


def expert_group(scal, loads, gate_pre, up_pre, w_gate, w_up, w_down, groups):
    _, slots, ffp = gate_pre.shape
    count = len(loads)
    tok = loads[0][0].shape[0] - 8
    width = w_gate.shape[0]
    chunk = width // 2

    def early(i):
        return jnp.minimum(i, 1)

    def late(i):
        return jnp.maximum(i - 2, 0)

    route = pl.BlockSpec((8, 4 * tok), lambda i, s: (tok // 8, 0))
    first = pl.BlockSpec((tok, chunk), lambda i, s: (0, 0))
    seconds = [
        pl.BlockSpec((tok, chunk), functools.partial(lambda i, s, skip: (0, skip), skip=b.shape[1] // chunk - 1))
        for a, b in loads
    ]
    pres = [
        pl.BlockSpec((1, slots, ffp), functools.partial(lambda i, s, n: (s[1 + n], 0, 0), n=n))
        for n in range(count)
    ]
    down = pl.BlockSpec((ffp, chunk), lambda i, s: (0, s[1 + count + early(i)]))
    up = pl.BlockSpec((chunk, ffp), lambda i, s: (late(i), 0))
    y = pl.BlockSpec((tok, chunk // 2), lambda i, s: (0, late(i)))
    half_rows = jax.ShapeDtypeStruct((tok, width // 2), BF16)
    m = count * slots
    outs = pl.pallas_call(
        functools.partial(expert_kernel, count=count, groups=groups, tok=tok, slots=slots),
        grid_spec=pltpu.PrefetchScalarGridSpec(
            num_scalar_prefetch=1,
            grid=(4,),
            in_specs=[route] * count + [first] * count + seconds + pres * 2 + [down, up, up],
            out_specs=[y] * (2 * count)
            + [
                pl.BlockSpec((m, chunk), lambda i, s: (0, s[1 + count + early(i)])),
                pl.BlockSpec((m, ffp), lambda i, s: (0, 0)),
                pl.BlockSpec((8, 128), lambda i, s: (0, 0)),
            ],
            scratch_shapes=[
                pltpu.VMEM((count, slots, tok), BF16),
                pltpu.VMEM((count, tok, slots), BF16),
                pltpu.VMEM((m, ffp), F32),
                pltpu.VMEM((m, ffp), BF16),
                pltpu.VMEM((m, ffp), BF16),
            ],
        ),
        out_shape=[half_rows] * (2 * count)
        + [
            jax.ShapeDtypeStruct((m, width), BF16),
            jax.ShapeDtypeStruct((m, ffp), BF16),
            jax.ShapeDtypeStruct((8, 128), F32),
        ],
        cost_estimate=pl.CostEstimate(
            flops=4 * m * width * (3 * ffp + 2 * tok), transcendentals=m * ffp, bytes_accessed=4 * m * width
        ),
        name="expert_group",
    )(
        scal,
        *[a for a, b in loads],
        *[a for a, b in loads],
        *[b for a, b in loads],
        *[gate_pre] * count,
        *[up_pre] * count,
        w_down,
        w_gate,
        w_up,
    )
    return outs[:count], outs[count : 2 * count], *outs[-3:]


def small_cost(us):
    return pl.CostEstimate(flops=int(us * 7e8), transcendentals=0, bytes_accessed=1 << 16)


def head_of(ref, h):
    return ref[:, h * HEAD_DIM : (h + 1) * HEAD_DIM]


def state_kernel(seg, left, right, out, *, edge, heads):
    keep = seg[...] == seg[edge : edge + 1, :]
    rows = jnp.where(keep, left[...].astype(F32), 0.0).astype(BF16)
    for h in range(heads):
        out[h] = dot(head_of(rows, h), head_of(right, h), (0, 0)).astype(BF16)


def columns(x, part, parts):
    return pl.BlockSpec((x.shape[0], x.shape[1] // parts), lambda i: (0, part))


def edge_state(seg_col, left, right, edge, part, parts):
    wide = left.shape[1] // parts
    heads = wide // HEAD_DIM
    whole = pl.BlockSpec((heads, HEAD_DIM, HEAD_DIM), lambda i: (0, 0, 0))
    right_parts = right.shape[1] // wide
    return pl.pallas_call(
        functools.partial(state_kernel, edge=edge, heads=heads),
        grid=(1,),
        in_specs=[columns(seg_col, 0, 1), columns(left, part, parts), columns(right, part % right_parts, right_parts)],
        out_specs=whole,
        out_shape=jax.ShapeDtypeStruct((heads, HEAD_DIM, HEAD_DIM), BF16),
        cost_estimate=small_cost(1),
        name="edge_state",
    )(seg_col, left, right)


def weighted(weights, side, states, shards):
    total = None
    for r in range(1, shards):
        w = weights[side : side + 1, r : r + 1]
        add = jnp.where(w[None] > 0.0, states[r][...].astype(F32), 0.0)
        total = add if total is None else total + add
    return total.astype(BF16)


def inner_kernel(weights, seg_col, seg_row, q, k, v, g, *refs, shards, tok, heads):
    states = (None, *refs[: shards - 1])
    dq, dk, dv = refs[-3:]
    col = seg_col[...]
    t_row = lax.broadcasted_iota(jnp.int32, (tok, tok), 0)
    t_col = lax.broadcasted_iota(jnp.int32, (tok, tok), 1)
    allowed = (t_row >= t_col) & (col == seg_row[...])
    before = col == col[:1, :]
    fwd = weighted(weights, 0, states, shards)
    for h in range(heads):
        qh, kh, vh, gh = head_of(q, h), head_of(k, h), head_of(v, h), head_of(g, h)
        here = pl.ds(h * HEAD_DIM, HEAD_DIM)
        cot_value = jnp.where(allowed, dot(gh, vh, (1, 1)), 0.0).astype(BF16)
        query_key = jnp.where(allowed, dot(qh, kh, (1, 1)), 0.0).astype(BF16)
        outer = jnp.where(before, dot(gh, fwd[h], (1, 1)), 0.0)
        dq[:, here] = (dot(cot_value, kh, (1, 0)) + outer).astype(BF16)
        dk[:, here] = dot(cot_value, qh, (0, 0))
        dv[:, here] = dot(query_key, gh, (0, 0))


def outer_kernel(weights, seg_col, k, v, dk_in, dv_in, *refs, shards, tok, heads):
    states = (None, *refs[: shards - 1])
    dk, dv = refs[-2:]
    col = seg_col[...]
    follow = col == col[tok - 1 :, :]
    back = weighted(weights, 1, states, shards)
    for h in range(heads):
        here = pl.ds(h * HEAD_DIM, HEAD_DIM)
        k_outer = jnp.where(follow, dot(head_of(v, h), back[h], (1, 1)), 0.0)
        v_outer = jnp.where(follow, dot(head_of(k, h), back[h], (1, 0)), 0.0)
        dk[:, here] = (dk_in[:, here] + k_outer).astype(BF16)
        dv[:, here] = (dv_in[:, here] + v_outer).astype(BF16)


def inner_grads(weights, seg_col, seg_row, q, k, v, g, states, part, parts, dq):
    tok, width = q.shape
    wide = width // parts
    heads = wide // HEAD_DIM
    shards = len(states) + 1
    mine = pl.BlockSpec((tok, wide), lambda i: (0, part))
    own = pl.BlockSpec((tok, wide), lambda i: (0, 0))
    state = pl.BlockSpec((heads, HEAD_DIM, HEAD_DIM), lambda i: (part, 0, 0))
    filled = [] if dq is None else [dq]
    return pl.pallas_call(
        functools.partial(inner_kernel, shards=shards, tok=tok, heads=heads),
        grid=(1,),
        in_specs=[
            pl.BlockSpec((8, 128), lambda i: (0, 0)),
            columns(seg_col, 0, 1),
            columns(seg_row, 0, 1),
            mine, mine, mine, own,
            *[state] * (shards - 1),
            *[pl.BlockSpec(memory_space=pl.ANY) for _ in filled],
        ],
        out_specs=[mine, own, own],
        out_shape=[
            jax.ShapeDtypeStruct((tok, width), BF16),
            jax.ShapeDtypeStruct((tok, wide), F32),
            jax.ShapeDtypeStruct((tok, wide), F32),
        ],
        input_output_aliases={6 + shards: 0} if filled else {},
        cost_estimate=small_cost(3),
        name="inner_grads",
    )(weights, seg_col, seg_row, q, k, v, g, *states, *filled)


def outer_grads(weights, seg_col, k, v, dk, dv, states, part, parts, filled):
    tok, width = k.shape
    wide = width // parts
    heads = wide // HEAD_DIM
    shards = len(states) + 1
    mine = pl.BlockSpec((tok, wide), lambda i: (0, part))
    own = pl.BlockSpec((tok, wide), lambda i: (0, 0))
    state = pl.BlockSpec((heads, HEAD_DIM, HEAD_DIM), lambda i: (0, 0, 0))
    return pl.pallas_call(
        functools.partial(outer_kernel, shards=shards, tok=tok, heads=heads),
        grid=(1,),
        in_specs=[
            pl.BlockSpec((8, 128), lambda i: (0, 0)),
            columns(seg_col, 0, 1),
            mine, mine, own, own,
            *[state] * (shards - 1),
            *[pl.BlockSpec(memory_space=pl.ANY) for _ in filled],
        ],
        out_specs=[mine, mine],
        out_shape=[jax.ShapeDtypeStruct((tok, width), BF16)] * 2,
        input_output_aliases={5 + shards: 0, 6 + shards: 1} if filled else {},
        cost_estimate=small_cost(2),
        name="outer_grads",
    )(weights, seg_col, k, v, dk, dv, *states, *filled)


def load_kernel(scal, rows, gates, ids, seg, load, half, seg_col, *, tok, width):
    start = pl.multiple_of(scal[0] * (width // 2), width // 2)
    load[:tok, :] = rows[...]
    half[:tok, :] = rows[:, pl.ds(start, width // 2)]
    gate_rows = gates[...].astype(F32)
    id_rows = ids[...].astype(F32)
    seg_rows = jnp.broadcast_to(seg[...].astype(F32), (128, tok))
    seg_col[...] = seg_rows.T[:, :1]
    rest = jnp.zeros((8, width // 2 - 3 * tok), F32)
    route = jnp.concatenate([gate_rows, id_rows, seg_rows[:8], rest], axis=1).astype(BF16)
    load[tok:, : width // 2] = route
    load[tok:, width // 2 :] = route
    half[tok:, :] = route


def make_load(parity, rows, gates, ids, seg):
    tok, width = rows.shape

    def whole(shape):
        return pl.BlockSpec(shape, lambda i, s: (0, 0))

    shapes = [(tok + 8, width), (tok + 8, width // 2), (tok, 1)]
    return pl.pallas_call(
        functools.partial(load_kernel, tok=tok, width=width),
        grid_spec=pltpu.PrefetchScalarGridSpec(
            num_scalar_prefetch=1,
            grid=(1,),
            in_specs=[whole(x.shape) for x in (rows, gates, ids, seg)],
            out_specs=[whole(x) for x in shapes],
        ),
        out_shape=[jax.ShapeDtypeStruct(x, t) for x, t in zip(shapes, (BF16, BF16, F32))],
        cost_estimate=small_cost(2),
        name="make_load",
    )(parity[None], rows, gates, ids, seg)


def weight_kernel(scal, *refs, shards, tok):
    routes, out = refs[:shards], refs[shards]
    me = scal[0]
    first = routes[0][:1, 2 * tok : 2 * tok + 1].astype(F32)
    last = routes[0][:1, 3 * tok - 1 : 3 * tok].astype(F32)
    side = lax.broadcasted_iota(jnp.int32, (8, 128), 0)
    lane = lax.broadcasted_iota(jnp.int32, (8, 128), 1)
    total = jnp.zeros((8, 128), F32)
    for r in range(1, shards):
        other = me ^ r
        first_r = routes[r][:1, 2 * tok : 2 * tok + 1].astype(F32)
        last_r = routes[r][:1, 3 * tok - 1 : 3 * tok].astype(F32)
        earlier = (last_r == first) & (other < me) & (side == 0)
        later = (first_r == last) & (other > me) & (side == 1)
        total = jnp.where((lane == r) & (earlier | later), 1.0, total)
    out[...] = total


def state_weights(me, loads, tok):
    shards = len(loads)
    return pl.pallas_call(
        functools.partial(weight_kernel, shards=shards, tok=tok),
        grid_spec=pltpu.PrefetchScalarGridSpec(
            num_scalar_prefetch=1,
            grid=(1,),
            in_specs=[pl.BlockSpec((8, 4 * tok), lambda i, s: (tok // 8, 0))] * shards,
            out_specs=pl.BlockSpec((8, 128), lambda i, s: (0, 0)),
        ),
        out_shape=jax.ShapeDtypeStruct((8, 128), F32),
        cost_estimate=small_cost(1),
        name="state_weights",
    )(me[None], *loads)


def all_states(own, chips):
    near = [own] + [swap(own, "ctx", 2 * j) for j in range(1, chips)]
    far = [swap(x, "ctx", 1) for x in near]
    return [(near if r % 2 == 0 else far)[r // 2] for r in range(1, 2 * chips)]


def local(
    out_grad, gate_values, expert_ids, segment_ids, gate_pre, up_pre, w_gate, w_up, w_down,
    queries, keys, values,
):
    shards = lax.axis_size("ctx")
    groups = lax.axis_size("ep")
    chips = shards // 2
    me = lax.axis_index("ctx").astype(jnp.int32)
    place = lax.axis_index("ep").astype(jnp.int32)
    parity = place % 2
    tok, width = out_grad.shape
    expert = 2 * me + place // (groups // 2)
    corners = [3] if chips == 4 else []
    sides = [j for j in range(1, chips) if j not in corners]
    weights3 = (w_gate[0], w_up[0], w_down[0])

    seg_row = segment_ids[None, :]
    load, mine, seg_col = make_load(parity, out_grad, gate_values.T, expert_ids.T, seg_row)
    seg_row = seg_row.astype(F32)
    near = {0: (load, load)}
    far = {}
    corner_half = {j: swap(mine, "ctx", 2 * j) for j in corners}
    far[0] = (swap(load, "ctx", 1),) * 2
    for j in sides:
        near[j] = (swap(load, "ctx", 2 * j),) * 2

    straight = [jnp.int32(0), jnp.int32(1)]
    turned = [parity, 1 - parity]

    def experts(js, order, token):
        loads, sources = [], []
        for j in js:
            loads += [near[j], far[j]]
            sources += [me ^ (2 * j), me ^ (2 * j + 1)]
        scal = jnp.stack([expert, *sources, *order])
        if token is not None:
            scal = after(scal, *token)
        low, high, cot, hidden, token = expert_group(
            scal, loads, gate_pre[0], up_pre[0], *weights3, groups
        )
        cots.append(cot)
        hiddens.append(hidden)
        for i, j in enumerate(js):
            sums[j] = tuple(
                (y[2 * i].astype(F32) + swap(y[2 * i + 1], "ctx", 1).astype(F32)).astype(BF16)
                for y in (low, high)
            )
        return [token]

    sums, cots, hiddens = {}, [], []
    token = experts([0], straight, None)
    for j in corners:
        ready = after(corner_half[j], *token)
        other_half = swap(ready, "ep", 1)
        near[j] = (ready, other_half)
        far[j] = (swap(ready, "ctx", 1), swap(other_half, "ctx", 1))
    for j in sides:
        far[j] = (swap(near[j][0], "ctx", 1),) * 2
    own = edge_state(after(seg_col, *token), keys, values, tok - 1, 0, 1)
    fwd = all_states(own, chips)
    for j in corners:
        token = experts([j], turned, token)
    extra = {}
    for j in corners:
        extra[2] = (swap(sums[j][0], "ctx", 2 * 1), None)
        extra[1] = (None, swap(sums[j][1], "ctx", 2 * 2))
        token = [*token, *sums[j]]
    for i in range(0, len(sides), 2):
        token = experts(sides[i : i + 2], straight, token)
    loads = [(near if r % 2 == 0 else far)[r // 2][0] for r in range(shards)]
    weights = state_weights(me, loads, tok)

    part = width // (2 * groups)
    totals, spreads = [], []
    for c in range(2):
        sends = []
        for j in sides:
            send = sums[j][c]
            if j in extra and extra[j][c] is not None:
                send = (send.astype(F32) + extra[j][c].astype(F32)).astype(BF16)
            sends.append(swap(send, "ctx", 2 * j))
        total = sums[0][c].astype(F32)
        sends = lax.optimization_barrier((*sends, *totals))[: len(sides)]
        for x in sends:
            total = total + x.astype(F32)
        total = total.astype(BF16)
        totals.append(total)
        pieces = []
        for j in range(1, groups):
            piece = lax.dynamic_slice_in_dim(total, (place ^ j) * part, part, 1)
            pieces.append(swap(piece, "ep", j))
        spreads.append(pieces)
    down_grad = dot(jnp.concatenate(hiddens), jnp.concatenate(cots), (0, 0))

    dq, dk_dv, before = None, [], [totals[1]]
    for c in range(2):
        pieces = lax.optimization_barrier((*spreads[c], *before))[: groups - 1]
        y_grad = lax.dynamic_slice_in_dim(totals[c], place * part, part, 1).astype(F32)
        for x in pieces:
            y_grad = y_grad + x.astype(F32)
        head_cot = y_grad.astype(BF16)
        own = edge_state(seg_col, queries, head_cot, 0, c, 2)
        back = all_states(own, chips)
        dq, dk, dv = inner_grads(
            weights, seg_col, seg_row, queries, keys, values, head_cot, fwd, c, 2, dq
        )
        before = [own, dk]
        dk_dv = outer_grads(weights, seg_col, keys, values, dk, dv, back, c, 2, dk_dv)
    return (dq, *dk_dv, down_grad[None])


def solution(mesh):
    return jax.shard_map(
        local,
        mesh=mesh,
        in_specs=(
            P("ctx", None),
            P("ctx", None),
            P("ctx", None),
            P("ctx"),
            P(("ctx", "ep"), None, None, None),
            P(("ctx", "ep"), None, None, None),
            P(("ctx", "ep"), None, None),
            P(("ctx", "ep"), None, None),
            P(("ctx", "ep"), None, None),
            P("ctx", "ep"),
            P("ctx", "ep"),
            P("ctx", "ep"),
        ),
        out_specs=(P("ctx", "ep"), P("ctx", "ep"), P("ctx", "ep"), P(("ctx", "ep"), None, None)),
        check_vma=False,
    )
```

```python
import functools

import jax
import jax.numpy as jnp
from jax import lax
from jax.experimental import pallas as pl
from jax.experimental.pallas import tpu as pltpu
from jax.sharding import PartitionSpec as P


HEAD_DIM = 128
BF16 = jnp.bfloat16
F32 = jnp.float32


def dot(a, b, dims):
    return lax.dot_general(a, b, ((dims[:1], dims[1:]), ((), ())), preferred_element_type=F32)


def swap(x, axis, offset):
    return lax.ppermute(x, axis, [(i, i ^ offset) for i in range(lax.axis_size(axis))])


def expert_kernel(scal, *refs, count, skip, groups, tok, slots):
    routes, refs = refs[:count], refs[count:]
    quarters, refs = [refs[q * count : (q + 1) * count] for q in range(4)], refs[4 * count :]
    pres, refs = refs[:count], refs[count:]
    ups, refs = refs[:count], refs[count:]
    w_down, w_gate, w_up = refs[:3]
    refs = refs[skip:]
    lows, highs = refs[3 : 3 + count], refs[3 + count : 3 + 2 * count]
    cot, hidden, token, pick, back, part, gate_delta, up_delta = refs[3 + 2 * count :]
    step = pl.program_id(0)

    @pl.when(step == 0)
    def _():
        token[...] = jnp.zeros_like(token)
        expert = scal[0].astype(F32)
        t_row = lax.broadcasted_iota(jnp.int32, (tok, tok), 0)
        t_col = lax.broadcasted_iota(jnp.int32, (tok, tok), 1)
        earlier = (t_row < t_col).astype(F32).astype(BF16)
        slot = lax.broadcasted_iota(jnp.int32, (slots, tok), 0)
        for i, route in enumerate(routes):
            gates = route[:, :tok].astype(F32)
            named = route[:, tok : 2 * tok].astype(F32) == expert
            gate = jnp.sum(jnp.where(named, gates, 0.0), axis=0, keepdims=True)
            mine = jnp.sum(named.astype(F32), axis=0, keepdims=True)
            spread = jnp.broadcast_to(mine, (8, tok)).astype(BF16)
            rank = dot(spread, earlier, (1, 0))[:1].astype(jnp.int32)
            chosen = jnp.where((slot == rank) & (mine > 0.0), 1.0, 0.0)
            pick[i] = (chosen * gate).astype(BF16)
            back[i] = chosen.T.astype(BF16)

    def gather(*rows):
        quarter = cot.shape[1] // 2
        for q in range(2):
            for i in range(count):
                here = (slice(i * slots, (i + 1) * slots), slice(q * quarter, (q + 1) * quarter))
                cot[here] = dot(pick[i], rows[q][i][...], (1, 0)).astype(BF16)
        return dot(cot[...], w_down[...], (1, 1))

    @pl.when(step == 0)
    def _():
        part[...] = gather(*quarters[:2])

    @pl.when(step == 1)
    def _():
        part[...] += gather(*quarters[2:])
        for i in range(count):
            here = pl.ds(i * slots, slots)
            a = pres[i][0].astype(F32)
            u = ups[i][0].astype(F32)
            s = jax.nn.sigmoid(a)
            d = part[here, :]
            hidden[here, :] = (a * s * u).astype(BF16)
            gate_delta[here, :] = (d * u * s * (1.0 + a * (1.0 - s))).astype(BF16)
            up_delta[here, :] = (d * a * s).astype(BF16)

    @pl.when(step >= 2)
    def _():
        both = dot(gate_delta[...], w_gate[...], (1, 1)) + dot(up_delta[...], w_up[...], (1, 1))
        both = both.astype(BF16)
        half = both.shape[1] // groups
        for i in range(count):
            y = dot(back[i], both[i * slots : (i + 1) * slots], (1, 0)).astype(BF16)
            for g in range(groups // 2):
                there = pl.ds(g * half, half)
                lows[i][:, there] = y[:, 2 * g * half : (2 * g + 1) * half]
                highs[i][:, there] = y[:, (2 * g + 1) * half : (2 * g + 2) * half]


def expert_group(scal, sources, order, tokens, loads, gate_pre, up_pre, weights, groups):
    _, slots, ffp = gate_pre.shape
    count = len(loads)
    tok = loads[0][0][0].shape[0] - 8
    width = weights[0].shape[1]
    chunk = width // 2

    def early(i):
        return jnp.minimum(i, 1)

    def late(i):
        return jnp.maximum(i - 2, 0)

    route = pl.BlockSpec((8, 2 * tok), lambda i, s: (tok // 8, 0))
    rows = [
        pl.BlockSpec((tok, chunk // 2), functools.partial(lambda i, s, block: (0, block), block=load[q][1]))
        for q in range(4)
        for load in loads
    ]
    pres = [
        pl.BlockSpec((1, slots, ffp), functools.partial(lambda i, s, n: (s[n], 0, 0), n=n))
        for n in sources
    ]
    down = pl.BlockSpec((ffp, chunk), lambda i, s: (0, s[order + early(i)]))
    up = pl.BlockSpec((chunk, ffp), lambda i, s: (late(i), 0))
    y = pl.BlockSpec((tok, chunk // 2), lambda i, s: (0, late(i)))
    half_rows = pltpu.HBM((tok, width // 2), BF16)
    m = count * slots
    outs = pl.pallas_call(
        functools.partial(expert_kernel, count=count, skip=len(tokens), groups=groups, tok=tok, slots=slots),
        grid_spec=pltpu.PrefetchScalarGridSpec(
            num_scalar_prefetch=1,
            grid=(4,),
            in_specs=[route] * count + rows + pres * 2 + [down, up, up] + [pl.BlockSpec(memory_space=pl.ANY)] * len(tokens),
            out_specs=[y] * (2 * count)
            + [
                pl.BlockSpec((m, chunk), lambda i, s: (0, s[order + early(i)])),
                pl.BlockSpec((m, ffp), lambda i, s: (0, 0)),
                pl.BlockSpec((8, 128), lambda i, s: (0, 0)),
            ],
            scratch_shapes=[
                pltpu.VMEM((count, slots, tok), BF16),
                pltpu.VMEM((count, tok, slots), BF16),
                pltpu.VMEM((m, ffp), F32),
                pltpu.VMEM((m, ffp), BF16),
                pltpu.VMEM((m, ffp), BF16),
            ],
        ),
        out_shape=[half_rows] * (2 * count)
        + [
            pltpu.HBM((m, width), BF16),
            pltpu.HBM((m, ffp), BF16),
            jax.ShapeDtypeStruct((8, 128), F32),
        ],
        cost_estimate=pl.CostEstimate(
            flops=4 * m * width * (3 * ffp + 2 * tok), transcendentals=m * ffp, bytes_accessed=4 * m * width
        ),
        compiler_params=pltpu.CompilerParams(vmem_limit_bytes=(4 + 13 * count) << 20),
        name="expert_group",
    )(
        scal,
        *[load[0][0] for load in loads],
        *[load[q][0] for q in range(4) for load in loads],
        *[pltpu.with_memory_space_constraint(gate_pre, pltpu.HBM)] * count,
        *[pltpu.with_memory_space_constraint(up_pre, pltpu.HBM)] * count,
        *weights,
        *tokens,
    )
    return outs[:count], outs[count : 2 * count], *outs[-3:]


def small_cost(us):
    return pl.CostEstimate(flops=int(us * 7e8), transcendentals=0, bytes_accessed=1 << 16)


def head_of(ref, h):
    return ref[:, h * HEAD_DIM : (h + 1) * HEAD_DIM]


def put_states(seg, left, right, out, edge, heads):
    keep = seg[...] == seg[edge : edge + 1, :]
    rows = jnp.where(keep, left[...].astype(F32), 0.0).astype(BF16)
    for h in range(heads):
        out[h] = dot(head_of(rows, h), right[:, h * HEAD_DIM : (h + 1) * HEAD_DIM], (0, 0)).astype(BF16)


def forward_kernel(seg, left, right, out, *, edge, heads):
    put_states(seg, left, right, out, edge, heads)


def backward_kernel(scal, seg, left, *refs, heads):
    right, out = refs[-2:]
    right[...] = sum(x[...].astype(F32) for x in refs[:-2]).astype(BF16)
    put_states(seg, left, right, out, 0, heads)


def columns(x, part, parts):
    return pl.BlockSpec((x.shape[0], x.shape[1] // parts), lambda i: (0, part))


def forward_states(seg_col, left, right):
    tok, width = left.shape
    heads = width // HEAD_DIM
    return pl.pallas_call(
        functools.partial(forward_kernel, edge=tok - 1, heads=heads),
        grid=(1,),
        in_specs=[columns(x, 0, 1) for x in (seg_col, left, right)],
        out_specs=pl.BlockSpec((heads, HEAD_DIM, HEAD_DIM), lambda i: (0, 0, 0)),
        out_shape=jax.ShapeDtypeStruct((heads, HEAD_DIM, HEAD_DIM), BF16),
        cost_estimate=small_cost(1),
        compiler_params=pltpu.CompilerParams(vmem_limit_bytes=8 << 20),
        name="forward_states",
    )(seg_col, left, right)


def backward_states(place, seg_col, left, total, pieces, part, parts):
    tok, width = left.shape
    wide = width // parts
    heads = wide // HEAD_DIM
    own = pl.BlockSpec((tok, wide), lambda i, s: (0, 0))
    return pl.pallas_call(
        functools.partial(backward_kernel, heads=heads),
        grid_spec=pltpu.PrefetchScalarGridSpec(
            num_scalar_prefetch=1,
            grid=(1,),
            in_specs=[
                pl.BlockSpec((tok, 1), lambda i, s: (0, 0)),
                pl.BlockSpec((tok, wide), lambda i, s: (0, part)),
                pl.BlockSpec((tok, wide), lambda i, s: (0, s[0])),
                *[own] * len(pieces),
            ],
            out_specs=[own, pl.BlockSpec((heads, HEAD_DIM, HEAD_DIM), lambda i, s: (0, 0, 0))],
        ),
        out_shape=[
            jax.ShapeDtypeStruct((tok, wide), BF16),
            jax.ShapeDtypeStruct((heads, HEAD_DIM, HEAD_DIM), BF16),
        ],
        cost_estimate=small_cost(1),
        compiler_params=pltpu.CompilerParams(vmem_limit_bytes=8 << 20),
        name="backward_states",
    )(place[None], seg_col, left, total, *pieces)


def weighted(weights, side, states, shards):
    total = None
    for r in range(1, shards):
        w = weights[side : side + 1, r : r + 1]
        add = jnp.where(w[None] > 0.0, states[r][...].astype(F32), 0.0)
        total = add if total is None else total + add
    return total.astype(BF16)


def inner_kernel(weights, seg_col, seg_row, q, k, v, g, *refs, shards, tok, heads):
    states = (None, *refs[: shards - 1])
    dq, dk, dv = refs[-3:]
    col = seg_col[...]
    t_row = lax.broadcasted_iota(jnp.int32, (tok, tok), 0)
    t_col = lax.broadcasted_iota(jnp.int32, (tok, tok), 1)
    allowed = (t_row >= t_col) & (col == seg_row[...])
    before = col == col[:1, :]
    fwd = weighted(weights, 0, states, shards)
    for h in range(heads):
        qh, kh, vh, gh = head_of(q, h), head_of(k, h), head_of(v, h), head_of(g, h)
        here = pl.ds(h * HEAD_DIM, HEAD_DIM)
        cot_value = jnp.where(allowed, dot(gh, vh, (1, 1)), 0.0).astype(BF16)
        query_key = jnp.where(allowed, dot(qh, kh, (1, 1)), 0.0).astype(BF16)
        outer = jnp.where(before, dot(gh, fwd[h], (1, 1)), 0.0)
        dq[:, here] = (dot(cot_value, kh, (1, 0)) + outer).astype(BF16)
        dk[:, here] = dot(cot_value, qh, (0, 0))
        dv[:, here] = dot(query_key, gh, (0, 0))


def outer_kernel(weights, seg_col, k, v, dk_in, dv_in, *refs, shards, tok, heads):
    states = (None, *refs[: shards - 1])
    dk, dv = refs[-2:]
    col = seg_col[...]
    follow = col == col[tok - 1 :, :]
    back = weighted(weights, 1, states, shards)
    for h in range(heads):
        here = pl.ds(h * HEAD_DIM, HEAD_DIM)
        k_outer = jnp.where(follow, dot(head_of(v, h), back[h], (1, 1)), 0.0)
        v_outer = jnp.where(follow, dot(head_of(k, h), back[h], (1, 0)), 0.0)
        dk[:, here] = (dk_in[:, here] + k_outer).astype(BF16)
        dv[:, here] = (dv_in[:, here] + v_outer).astype(BF16)


def inner_grads(weights, seg_col, seg_row, q, k, v, g, states, part, parts, dq):
    tok, width = q.shape
    wide = width // parts
    heads = wide // HEAD_DIM
    shards = len(states) + 1
    mine = pl.BlockSpec((tok, wide), lambda i: (0, part))
    own = pl.BlockSpec((tok, wide), lambda i: (0, 0))
    state = pl.BlockSpec((heads, HEAD_DIM, HEAD_DIM), lambda i: (part, 0, 0))
    filled = [] if dq is None else [dq]
    return pl.pallas_call(
        functools.partial(inner_kernel, shards=shards, tok=tok, heads=heads),
        grid=(1,),
        in_specs=[
            pl.BlockSpec((8, 128), lambda i: (0, 0)),
            columns(seg_col, 0, 1),
            columns(seg_row, 0, 1),
            mine, mine, mine, own,
            *[state] * (shards - 1),
            *[pl.BlockSpec(memory_space=pl.ANY) for _ in filled],
        ],
        out_specs=[mine, own, own],
        out_shape=[
            jax.ShapeDtypeStruct((tok, width), BF16),
            jax.ShapeDtypeStruct((tok, wide), F32),
            jax.ShapeDtypeStruct((tok, wide), F32),
        ],
        input_output_aliases={6 + shards: 0} if filled else {},
        cost_estimate=small_cost(3),
        compiler_params=pltpu.CompilerParams(vmem_limit_bytes=8 << 20),
        name="inner_grads",
    )(weights, seg_col, seg_row, q, k, v, g, *states, *filled)


def outer_grads(weights, seg_col, k, v, dk, dv, states, part, parts, filled):
    tok, width = k.shape
    wide = width // parts
    heads = wide // HEAD_DIM
    shards = len(states) + 1
    mine = pl.BlockSpec((tok, wide), lambda i: (0, part))
    own = pl.BlockSpec((tok, wide), lambda i: (0, 0))
    state = pl.BlockSpec((heads, HEAD_DIM, HEAD_DIM), lambda i: (0, 0, 0))
    return pl.pallas_call(
        functools.partial(outer_kernel, shards=shards, tok=tok, heads=heads),
        grid=(1,),
        in_specs=[
            pl.BlockSpec((8, 128), lambda i: (0, 0)),
            columns(seg_col, 0, 1),
            mine, mine, own, own,
            *[state] * (shards - 1),
            *[pl.BlockSpec(memory_space=pl.ANY) for _ in filled],
        ],
        out_specs=[mine, mine],
        out_shape=[jax.ShapeDtypeStruct((tok, width), BF16)] * 2,
        input_output_aliases={5 + shards: 0, 6 + shards: 1} if filled else {},
        cost_estimate=small_cost(2),
        compiler_params=pltpu.CompilerParams(vmem_limit_bytes=8 << 20),
        name="outer_grads",
    )(weights, seg_col, k, v, dk, dv, *states, *filled)


def load_kernel(scal, rows, gates, ids, seg, load, low, high, seg_col, seg_row, *, tok, width):
    quarter = width // 4
    start = pl.multiple_of(scal[0] * 2 * quarter, 2 * quarter)
    load[:tok, :] = rows[...]
    low[:tok, :] = rows[:, pl.ds(start, quarter)]
    high[:tok, :] = rows[:, pl.ds(start + quarter, quarter)]
    segment = seg[...].astype(F32)
    seg_rows = jnp.broadcast_to(segment, (128, tok))
    seg_col[...] = seg_rows.T[:, :1]
    seg_row[...] = segment

    def padded(*parts):
        spare = quarter - sum(x.shape[1] for x in parts)
        parts += (jnp.zeros((8, spare), F32),) if spare else ()
        return jnp.concatenate(parts, axis=1).astype(BF16)

    route = padded(gates[...].astype(F32), ids[...].astype(F32))
    seg_part = padded(seg_rows[:8])
    for q in range(4):
        load[tok:, q * quarter : (q + 1) * quarter] = seg_part if q % 2 else route
    low[tok:, :] = route
    high[tok:, :] = seg_part


def make_load(parity, rows, gates, ids, seg):
    tok, width = rows.shape

    def whole(shape):
        return pl.BlockSpec(shape, lambda i, s: (0, 0))

    shapes = [(tok + 8, width), (tok + 8, width // 4), (tok + 8, width // 4), (tok, 1), (1, tok)]
    return pl.pallas_call(
        functools.partial(load_kernel, tok=tok, width=width),
        grid_spec=pltpu.PrefetchScalarGridSpec(
            num_scalar_prefetch=1,
            grid=(1,),
            in_specs=[whole(x.shape) for x in (rows, gates, ids, seg)],
            out_specs=[whole(x) for x in shapes],
        ),
        out_shape=[jax.ShapeDtypeStruct(x, t) for x, t in zip(shapes, (BF16, BF16, BF16, F32, F32))],
        cost_estimate=small_cost(2),
        name="make_load",
    )(parity[None], rows, gates, ids, seg)


def weight_kernel(scal, *refs, shards, tok):
    routes, out = refs[:shards], refs[shards]
    me = scal[0]
    first = routes[0][:1, :1].astype(F32)
    last = routes[0][:1, tok - 1 : tok].astype(F32)
    side = lax.broadcasted_iota(jnp.int32, (8, 128), 0)
    lane = lax.broadcasted_iota(jnp.int32, (8, 128), 1)
    total = jnp.zeros((8, 128), F32)
    for r in range(1, shards):
        other = me ^ r
        first_r = routes[r][:1, :1].astype(F32)
        last_r = routes[r][:1, tok - 1 : tok].astype(F32)
        earlier = (last_r == first) & (other < me) & (side == 0)
        later = (first_r == last) & (other > me) & (side == 1)
        total = jnp.where((lane == r) & (earlier | later), 1.0, total)
    out[...] = total


def state_weights(me, loads, tok):
    shards = len(loads)
    return pl.pallas_call(
        functools.partial(weight_kernel, shards=shards, tok=tok),
        grid_spec=pltpu.PrefetchScalarGridSpec(
            num_scalar_prefetch=1,
            grid=(1,),
            in_specs=[
                pl.BlockSpec(
                    (8, tok), functools.partial(lambda i, s, block: (tok // 8, block), block=b // tok)
                )
                for x, b in loads
            ],
            out_specs=pl.BlockSpec((8, 128), lambda i, s: (0, 0)),
        ),
        out_shape=jax.ShapeDtypeStruct((8, 128), F32),
        cost_estimate=small_cost(1),
        compiler_params=pltpu.CompilerParams(vmem_limit_bytes=8 << 20),
        name="state_weights",
    )(me[None], *[x for x, b in loads])


def near_states(own, chips):
    return [own] + [swap(own, "ctx", 2 * j) for j in range(1, chips)]


def all_states(near):
    far = [swap(x, "ctx", 1) for x in near]
    return [(near if r % 2 == 0 else far)[r // 2] for r in range(1, 2 * len(near))]


def local(
    out_grad, gate_values, expert_ids, segment_ids, gate_pre, up_pre, w_gate, w_up, w_down,
    queries, keys, values,
):
    shards = lax.axis_size("ctx")
    groups = lax.axis_size("ep")
    chips = shards // 2
    me = lax.axis_index("ctx").astype(jnp.int32)
    place = lax.axis_index("ep").astype(jnp.int32)
    parity = place % 2
    tok, width = out_grad.shape
    expert = 2 * me + place // (groups // 2)
    corners = [3] if chips == 4 else []
    sides = [j for j in range(1, chips) if j not in corners]
    weights3 = [pltpu.with_memory_space_constraint(x[0], pltpu.VMEM) for x in (w_down, w_gate, w_up)]

    load, low, high, seg_col, seg_row = make_load(
        parity, out_grad, gate_values.T, expert_ids.T, segment_ids[None, :]
    )

    def whole(x):
        return [(x, q) for q in range(4)]

    near, far = {0: whole(load)}, {}
    corner_half = {j: [swap(x, "ctx", 2 * j) for x in (low, high)] for j in corners}
    far[0] = whole(swap(load, "ctx", 1))
    for j in sides:
        near[j] = whole(swap(load, "ctx", 2 * j))

    scal = jnp.stack([expert] + [me ^ r for r in range(shards)] + [me * 0, me * 0 + 1, parity, 1 - parity])
    straight, turned = shards + 1, shards + 3

    def experts(js, order, tokens):
        loads, sources = [], []
        for j in js:
            loads += [near[j], far[j]]
            sources += [1 + 2 * j, 2 + 2 * j]
        low, high, cot, hidden, token = expert_group(
            scal, sources, order, tokens, loads, gate_pre[0], up_pre[0], weights3, groups
        )
        cots.append(cot)
        hiddens.append(hidden)
        for i, j in enumerate(js):
            sums[j] = [[y[2 * i], swap(y[2 * i + 1], "ctx", 1)] for y in (low, high)]
        return [token]

    def added(xs):
        return sum(x.astype(F32) for x in xs).astype(BF16)

    sums, cots, hiddens = {}, [], []
    for j in corners:
        first, second = corner_half[j]
        third = swap(first, "ep", 1)
        fourth = swap(second, "ep", 1)
        near[j] = [(x, 0) for x in (first, second, third, fourth)]
        far[j] = [(swap(x, "ctx", 1), 0) for x, _ in near[j]]
    for j in sides:
        far[j] = whole(swap(near[j][0][0], "ctx", 1))
    own = forward_states(seg_col, keys, values)
    fwd_near = near_states(own, chips)
    token = experts([0], straight, [])
    for j in corners:
        token = experts([j], turned, token)
    extra = {}
    for i, j in enumerate(sides):
        token = experts([j], straight, token)
        if i == 0:
            for k in corners:
                rows = [added(lax.optimization_barrier((*x, *token))[:2]) for x in sums[k]]
                extra[2] = ([swap(rows[0], "ctx", 2 * 1)], [])
                extra[1] = ([], [swap(rows[1], "ctx", 2 * 2)])
                token = [*token, *rows]
    loads = [(near if r % 2 == 0 else far)[r // 2][1] for r in range(shards)]
    weights = state_weights(me, [(x, b * (width // 4)) for x, b in loads], tok)

    part = width // (2 * groups)
    totals, spreads = [], []
    for c in range(2):
        rows = [added(sums[j][c] + extra.get(j, ([], []))[c]) for j in sides]
        sends = [swap(x, "ctx", 2 * j) for j, x in zip(sides, rows)]
        total = sums[0][c][0].astype(F32) + sums[0][c][1].astype(F32)
        sends = lax.optimization_barrier((*sends, *totals))[: len(sides)]
        for x in sends:
            total = total + x.astype(F32)
        total = total.astype(BF16)
        totals.append(total)
        pieces = []
        for j in range(1, groups):
            piece = lax.dynamic_slice_in_dim(total, (place ^ j) * part, part, 1)
            pieces.append(swap(piece, "ep", j))
        spreads.append(pieces)
    down_grad = dot(jnp.concatenate(hiddens), jnp.concatenate(cots), (0, 0))

    fwd = all_states(lax.optimization_barrier((*fwd_near, totals[1]))[:chips])
    dq, dk_dv, before = None, [], [totals[1]]
    for c in range(2):
        pieces = lax.optimization_barrier((*spreads[c], *before))[: groups - 1]
        head_cot, own = backward_states(place, seg_col, queries, totals[c], pieces, c, 2)
        back = all_states(near_states(own, chips))
        dq, dk, dv = inner_grads(
            weights, seg_col, seg_row, queries, keys, values, head_cot, fwd, c, 2, dq
        )
        before = [own, dk]
        dk_dv = outer_grads(weights, seg_col, keys, values, dk, dv, back, c, 2, dk_dv)
    return (dq, *dk_dv, down_grad[None])


def solution(mesh):
    return jax.shard_map(
        local,
        mesh=mesh,
        in_specs=(
            P("ctx", None),
            P("ctx", None),
            P("ctx", None),
            P("ctx"),
            P(("ctx", "ep"), None, None, None),
            P(("ctx", "ep"), None, None, None),
            P(("ctx", "ep"), None, None),
            P(("ctx", "ep"), None, None),
            P(("ctx", "ep"), None, None),
            P("ctx", "ep"),
            P("ctx", "ep"),
            P("ctx", "ep"),
        ),
        out_specs=(P("ctx", "ep"), P("ctx", "ep"), P("ctx", "ep"), P(("ctx", "ep"), None, None)),
        check_vma=False,
    )
```

```python
import functools

import jax
import jax.numpy as jnp
from jax import lax
from jax.experimental import pallas as pl
from jax.experimental.pallas import tpu as pltpu
from jax.sharding import PartitionSpec as P


HEAD_DIM = 128
BF16 = jnp.bfloat16
F32 = jnp.float32


def dot(a, b, dims):
    return lax.dot_general(a, b, ((dims[:1], dims[1:]), ((), ())), preferred_element_type=F32)


def swap(x, axis, offset):
    return lax.ppermute(x, axis, [(i, i ^ offset) for i in range(lax.axis_size(axis))])


def expert_kernel(scal, *refs, count, skip, groups, tok, slots):
    routes, refs = refs[:count], refs[count:]
    quarters, refs = [refs[q * count : (q + 1) * count] for q in range(4)], refs[4 * count :]
    pres, refs = refs[:count], refs[count:]
    ups, refs = refs[:count], refs[count:]
    w_down, w_gate, w_up = refs[:3]
    refs = refs[skip:]
    lows, highs = refs[3 : 3 + count], refs[3 + count : 3 + 2 * count]
    cot, hidden, token, pick, back, part, gate_delta, up_delta = refs[3 + 2 * count :]
    step = pl.program_id(0)

    @pl.when(step == 0)
    def _():
        token[...] = jnp.zeros_like(token)
        expert = scal[0].astype(F32)
        t_row = lax.broadcasted_iota(jnp.int32, (tok, tok), 0)
        t_col = lax.broadcasted_iota(jnp.int32, (tok, tok), 1)
        earlier = (t_row < t_col).astype(F32).astype(BF16)
        slot = lax.broadcasted_iota(jnp.int32, (slots, tok), 0)
        for i, route in enumerate(routes):
            gates = route[:, :tok].astype(F32)
            named = route[:, tok : 2 * tok].astype(F32) == expert
            gate = jnp.sum(jnp.where(named, gates, 0.0), axis=0, keepdims=True)
            mine = jnp.sum(named.astype(F32), axis=0, keepdims=True)
            spread = jnp.broadcast_to(mine, (8, tok)).astype(BF16)
            rank = dot(spread, earlier, (1, 0))[:1].astype(jnp.int32)
            chosen = jnp.where((slot == rank) & (mine > 0.0), 1.0, 0.0)
            pick[i] = (chosen * gate).astype(BF16)
            back[i] = chosen.T.astype(BF16)

    def gather(*rows):
        quarter = cot.shape[1] // 2
        for q in range(2):
            for i in range(count):
                here = (slice(i * slots, (i + 1) * slots), slice(q * quarter, (q + 1) * quarter))
                cot[here] = dot(pick[i], rows[q][i][...], (1, 0)).astype(BF16)
        return dot(cot[...], w_down[...], (1, 1))

    @pl.when(step == 0)
    def _():
        part[...] = gather(*quarters[:2])

    @pl.when(step == 1)
    def _():
        part[...] += gather(*quarters[2:])
        for i in range(count):
            here = pl.ds(i * slots, slots)
            a = pres[i][0].astype(F32)
            u = ups[i][0].astype(F32)
            s = jax.nn.sigmoid(a)
            d = part[here, :]
            hidden[here, :] = (a * s * u).astype(BF16)
            gate_delta[here, :] = (d * u * s * (1.0 + a * (1.0 - s))).astype(BF16)
            up_delta[here, :] = (d * a * s).astype(BF16)

    @pl.when(step >= 2)
    def _():
        both = dot(gate_delta[...], w_gate[...], (1, 1)) + dot(up_delta[...], w_up[...], (1, 1))
        both = both.astype(BF16)
        half = both.shape[1] // groups
        for i in range(count):
            y = dot(back[i], both[i * slots : (i + 1) * slots], (1, 0)).astype(BF16)
            for g in range(groups // 2):
                there = pl.ds(g * half, half)
                lows[i][:, there] = y[:, 2 * g * half : (2 * g + 1) * half]
                highs[i][:, there] = y[:, (2 * g + 1) * half : (2 * g + 2) * half]


def expert_group(scal, sources, order, tokens, loads, gate_pre, up_pre, weights, groups):
    _, slots, ffp = gate_pre.shape
    count = len(loads)
    tok = loads[0][0][0].shape[0] - 8
    width = weights[0].shape[1]
    chunk = width // 2

    def early(i):
        return jnp.minimum(i, 1)

    def late(i):
        return jnp.maximum(i - 2, 0)

    route = pl.BlockSpec((8, 2 * tok), lambda i, s: (tok // 8, 0))
    rows = [
        pl.BlockSpec((tok, chunk // 2), functools.partial(lambda i, s, block: (0, block), block=load[q][1]))
        for q in range(4)
        for load in loads
    ]
    pres = [
        pl.BlockSpec((1, slots, ffp), functools.partial(lambda i, s, n: (s[n], 0, 0), n=n))
        for n in sources
    ]
    down = pl.BlockSpec((ffp, chunk), lambda i, s: (0, s[order + early(i)]))
    up = pl.BlockSpec((chunk, ffp), lambda i, s: (late(i), 0))
    y = pl.BlockSpec((tok, chunk // 2), lambda i, s: (0, late(i)))
    half_rows = pltpu.HBM((tok, width // 2), BF16)
    m = count * slots
    outs = pl.pallas_call(
        functools.partial(expert_kernel, count=count, skip=len(tokens), groups=groups, tok=tok, slots=slots),
        grid_spec=pltpu.PrefetchScalarGridSpec(
            num_scalar_prefetch=1,
            grid=(4,),
            in_specs=[route] * count + rows + pres * 2 + [down, up, up] + [pl.BlockSpec(memory_space=pl.ANY)] * len(tokens),
            out_specs=[y] * (2 * count)
            + [
                pl.BlockSpec((m, chunk), lambda i, s: (0, s[order + early(i)])),
                pl.BlockSpec((m, ffp), lambda i, s: (0, 0)),
                pl.BlockSpec((8, 128), lambda i, s: (0, 0)),
            ],
            scratch_shapes=[
                pltpu.VMEM((count, slots, tok), BF16),
                pltpu.VMEM((count, tok, slots), BF16),
                pltpu.VMEM((m, ffp), F32),
                pltpu.VMEM((m, ffp), BF16),
                pltpu.VMEM((m, ffp), BF16),
            ],
        ),
        out_shape=[half_rows] * (2 * count)
        + [
            pltpu.HBM((m, width), BF16),
            pltpu.HBM((m, ffp), BF16),
            jax.ShapeDtypeStruct((8, 128), F32),
        ],
        cost_estimate=pl.CostEstimate(
            flops=4 * m * width * (3 * ffp + 2 * tok), transcendentals=m * ffp, bytes_accessed=4 * m * width
        ),
        compiler_params=pltpu.CompilerParams(vmem_limit_bytes=(4 + 13 * count) << 20),
    )(
        scal,
        *[load[0][0] for load in loads],
        *[load[q][0] for q in range(4) for load in loads],
        *[pltpu.with_memory_space_constraint(gate_pre, pltpu.HBM)] * count,
        *[pltpu.with_memory_space_constraint(up_pre, pltpu.HBM)] * count,
        *weights,
        *tokens,
    )
    return outs[:count], outs[count : 2 * count], *outs[-3:]


def small_cost(us):
    return pl.CostEstimate(flops=int(us * 7e8), transcendentals=0, bytes_accessed=1 << 16)


def head_of(ref, h):
    return ref[:, h * HEAD_DIM : (h + 1) * HEAD_DIM]


def put_states(seg, left, right, out, edge, heads):
    keep = seg[...] == seg[edge : edge + 1, :]
    rows = jnp.where(keep, left[...].astype(F32), 0.0).astype(BF16)
    for h in range(heads):
        out[h] = dot(head_of(rows, h), right[:, h * HEAD_DIM : (h + 1) * HEAD_DIM], (0, 0)).astype(BF16)


def forward_kernel(seg, left, right, out, *, edge, heads):
    put_states(seg, left, right, out, edge, heads)


def backward_kernel(scal, seg, left, *refs, heads):
    right, out = refs[-2:]
    right[...] = sum(x[...].astype(F32) for x in refs[:-2]).astype(BF16)
    put_states(seg, left, right, out, 0, heads)


def columns(x, part, parts):
    return pl.BlockSpec((x.shape[0], x.shape[1] // parts), lambda i: (0, part))


def forward_states(seg_col, left, right):
    tok, width = left.shape
    heads = width // HEAD_DIM
    return pl.pallas_call(
        functools.partial(forward_kernel, edge=tok - 1, heads=heads),
        grid=(1,),
        in_specs=[columns(x, 0, 1) for x in (seg_col, left, right)],
        out_specs=pl.BlockSpec((heads, HEAD_DIM, HEAD_DIM), lambda i: (0, 0, 0)),
        out_shape=jax.ShapeDtypeStruct((heads, HEAD_DIM, HEAD_DIM), BF16),
        cost_estimate=small_cost(1),
        compiler_params=pltpu.CompilerParams(vmem_limit_bytes=8 << 20),
    )(seg_col, left, right)


def backward_states(place, seg_col, left, total, pieces, part, parts):
    tok, width = left.shape
    wide = width // parts
    heads = wide // HEAD_DIM
    own = pl.BlockSpec((tok, wide), lambda i, s: (0, 0))
    return pl.pallas_call(
        functools.partial(backward_kernel, heads=heads),
        grid_spec=pltpu.PrefetchScalarGridSpec(
            num_scalar_prefetch=1,
            grid=(1,),
            in_specs=[
                pl.BlockSpec((tok, 1), lambda i, s: (0, 0)),
                pl.BlockSpec((tok, wide), lambda i, s: (0, part)),
                pl.BlockSpec((tok, wide), lambda i, s: (0, s[0])),
                *[own] * len(pieces),
            ],
            out_specs=[own, pl.BlockSpec((heads, HEAD_DIM, HEAD_DIM), lambda i, s: (0, 0, 0))],
        ),
        out_shape=[
            jax.ShapeDtypeStruct((tok, wide), BF16),
            jax.ShapeDtypeStruct((heads, HEAD_DIM, HEAD_DIM), BF16),
        ],
        cost_estimate=small_cost(1),
        compiler_params=pltpu.CompilerParams(vmem_limit_bytes=8 << 20),
    )(place[None], seg_col, left, total, *pieces)


def weighted(weights, side, states, shards):
    total = None
    for r in range(1, shards):
        w = weights[side : side + 1, r : r + 1]
        add = jnp.where(w[None] > 0.0, states[r][...].astype(F32), 0.0)
        total = add if total is None else total + add
    return total.astype(BF16)


def inner_kernel(weights, seg_col, seg_row, q, k, v, g, *refs, shards, tok, heads):
    states = (None, *refs[: shards - 1])
    dq, dk, dv = refs[-3:]
    col = seg_col[...]
    t_row = lax.broadcasted_iota(jnp.int32, (tok, tok), 0)
    t_col = lax.broadcasted_iota(jnp.int32, (tok, tok), 1)
    allowed = (t_row >= t_col) & (col == seg_row[...])
    before = col == col[:1, :]
    fwd = weighted(weights, 0, states, shards)
    for h in range(heads):
        qh, kh, vh, gh = head_of(q, h), head_of(k, h), head_of(v, h), head_of(g, h)
        here = pl.ds(h * HEAD_DIM, HEAD_DIM)
        cot_value = jnp.where(allowed, dot(gh, vh, (1, 1)), 0.0).astype(BF16)
        query_key = jnp.where(allowed, dot(qh, kh, (1, 1)), 0.0).astype(BF16)
        outer = jnp.where(before, dot(gh, fwd[h], (1, 1)), 0.0)
        dq[:, here] = (dot(cot_value, kh, (1, 0)) + outer).astype(BF16)
        dk[:, here] = dot(cot_value, qh, (0, 0))
        dv[:, here] = dot(query_key, gh, (0, 0))


def outer_kernel(weights, seg_col, k, v, dk_in, dv_in, *refs, shards, tok, heads):
    states = (None, *refs[: shards - 1])
    dk, dv = refs[-2:]
    col = seg_col[...]
    follow = col == col[tok - 1 :, :]
    back = weighted(weights, 1, states, shards)
    for h in range(heads):
        here = pl.ds(h * HEAD_DIM, HEAD_DIM)
        k_outer = jnp.where(follow, dot(head_of(v, h), back[h], (1, 1)), 0.0)
        v_outer = jnp.where(follow, dot(head_of(k, h), back[h], (1, 0)), 0.0)
        dk[:, here] = (dk_in[:, here] + k_outer).astype(BF16)
        dv[:, here] = (dv_in[:, here] + v_outer).astype(BF16)


def inner_grads(weights, seg_col, seg_row, q, k, v, g, states, part, parts, dq):
    tok, width = q.shape
    wide = width // parts
    heads = wide // HEAD_DIM
    shards = len(states) + 1
    mine = pl.BlockSpec((tok, wide), lambda i: (0, part))
    own = pl.BlockSpec((tok, wide), lambda i: (0, 0))
    state = pl.BlockSpec((heads, HEAD_DIM, HEAD_DIM), lambda i: (part, 0, 0))
    filled = [] if dq is None else [dq]
    return pl.pallas_call(
        functools.partial(inner_kernel, shards=shards, tok=tok, heads=heads),
        grid=(1,),
        in_specs=[
            pl.BlockSpec((8, 128), lambda i: (0, 0)),
            columns(seg_col, 0, 1),
            columns(seg_row, 0, 1),
            mine, mine, mine, own,
            *[state] * (shards - 1),
            *[pl.BlockSpec(memory_space=pl.ANY) for _ in filled],
        ],
        out_specs=[mine, own, own],
        out_shape=[
            jax.ShapeDtypeStruct((tok, width), BF16),
            jax.ShapeDtypeStruct((tok, wide), F32),
            jax.ShapeDtypeStruct((tok, wide), F32),
        ],
        input_output_aliases={6 + shards: 0} if filled else {},
        cost_estimate=small_cost(3),
        compiler_params=pltpu.CompilerParams(vmem_limit_bytes=8 << 20),
    )(weights, seg_col, seg_row, q, k, v, g, *states, *filled)


def outer_grads(weights, seg_col, k, v, dk, dv, states, part, parts, filled):
    tok, width = k.shape
    wide = width // parts
    heads = wide // HEAD_DIM
    shards = len(states) + 1
    mine = pl.BlockSpec((tok, wide), lambda i: (0, part))
    own = pl.BlockSpec((tok, wide), lambda i: (0, 0))
    state = pl.BlockSpec((heads, HEAD_DIM, HEAD_DIM), lambda i: (0, 0, 0))
    return pl.pallas_call(
        functools.partial(outer_kernel, shards=shards, tok=tok, heads=heads),
        grid=(1,),
        in_specs=[
            pl.BlockSpec((8, 128), lambda i: (0, 0)),
            columns(seg_col, 0, 1),
            mine, mine, own, own,
            *[state] * (shards - 1),
            *[pl.BlockSpec(memory_space=pl.ANY) for _ in filled],
        ],
        out_specs=[mine, mine],
        out_shape=[jax.ShapeDtypeStruct((tok, width), BF16)] * 2,
        input_output_aliases={5 + shards: 0, 6 + shards: 1} if filled else {},
        cost_estimate=small_cost(2),
        compiler_params=pltpu.CompilerParams(vmem_limit_bytes=8 << 20),
    )(weights, seg_col, k, v, dk, dv, *states, *filled)


def load_kernel(scal, rows, gates, ids, seg, load, low, high, seg_col, seg_row, *, tok, width):
    quarter = width // 4
    start = pl.multiple_of(scal[0] * 2 * quarter, 2 * quarter)
    load[:tok, :] = rows[...]
    low[:tok, :] = rows[:, pl.ds(start, quarter)]
    high[:tok, :] = rows[:, pl.ds(start + quarter, quarter)]
    segment = seg[...].astype(F32)
    seg_rows = jnp.broadcast_to(segment, (128, tok))
    seg_col[...] = seg_rows.T[:, :1]
    seg_row[...] = segment

    def padded(*parts):
        spare = quarter - sum(x.shape[1] for x in parts)
        parts += (jnp.zeros((8, spare), F32),) if spare else ()
        return jnp.concatenate(parts, axis=1).astype(BF16)

    route = padded(gates[...].astype(F32), ids[...].astype(F32))
    seg_part = padded(seg_rows[:8])
    for q in range(4):
        load[tok:, q * quarter : (q + 1) * quarter] = seg_part if q % 2 else route
    low[tok:, :] = route
    high[tok:, :] = seg_part


def make_load(parity, rows, gates, ids, seg):
    tok, width = rows.shape

    def whole(shape):
        return pl.BlockSpec(shape, lambda i, s: (0, 0))

    shapes = [(tok + 8, width), (tok + 8, width // 4), (tok + 8, width // 4), (tok, 1), (1, tok)]
    return pl.pallas_call(
        functools.partial(load_kernel, tok=tok, width=width),
        grid_spec=pltpu.PrefetchScalarGridSpec(
            num_scalar_prefetch=1,
            grid=(1,),
            in_specs=[whole(x.shape) for x in (rows, gates, ids, seg)],
            out_specs=[whole(x) for x in shapes],
        ),
        out_shape=[jax.ShapeDtypeStruct(x, t) for x, t in zip(shapes, (BF16, BF16, BF16, F32, F32))],
        cost_estimate=small_cost(2),
    )(parity[None], rows, gates, ids, seg)


def weight_kernel(scal, *refs, shards, tok):
    routes, out = refs[:shards], refs[shards]
    me = scal[0]
    first = routes[0][:1, :1].astype(F32)
    last = routes[0][:1, tok - 1 : tok].astype(F32)
    side = lax.broadcasted_iota(jnp.int32, (8, 128), 0)
    lane = lax.broadcasted_iota(jnp.int32, (8, 128), 1)
    total = jnp.zeros((8, 128), F32)
    for r in range(1, shards):
        other = me ^ r
        first_r = routes[r][:1, :1].astype(F32)
        last_r = routes[r][:1, tok - 1 : tok].astype(F32)
        earlier = (last_r == first) & (other < me) & (side == 0)
        later = (first_r == last) & (other > me) & (side == 1)
        total = jnp.where((lane == r) & (earlier | later), 1.0, total)
    out[...] = total


def state_weights(me, loads, tok):
    shards = len(loads)
    return pl.pallas_call(
        functools.partial(weight_kernel, shards=shards, tok=tok),
        grid_spec=pltpu.PrefetchScalarGridSpec(
            num_scalar_prefetch=1,
            grid=(1,),
            in_specs=[
                pl.BlockSpec(
                    (8, tok), functools.partial(lambda i, s, block: (tok // 8, block), block=b // tok)
                )
                for x, b in loads
            ],
            out_specs=pl.BlockSpec((8, 128), lambda i, s: (0, 0)),
        ),
        out_shape=jax.ShapeDtypeStruct((8, 128), F32),
        cost_estimate=small_cost(1),
        compiler_params=pltpu.CompilerParams(vmem_limit_bytes=8 << 20),
    )(me[None], *[x for x, b in loads])


def near_states(own, chips):
    return [own] + [swap(own, "ctx", 2 * j) for j in range(1, chips)]


def all_states(near):
    far = [swap(x, "ctx", 1) for x in near]
    return [(near if r % 2 == 0 else far)[r // 2] for r in range(1, 2 * len(near))]


def local(
    out_grad, gate_values, expert_ids, segment_ids, gate_pre, up_pre, w_gate, w_up, w_down,
    queries, keys, values,
):
    shards = lax.axis_size("ctx")
    groups = lax.axis_size("ep")
    chips = shards // 2
    me = lax.axis_index("ctx").astype(jnp.int32)
    place = lax.axis_index("ep").astype(jnp.int32)
    parity = place % 2
    tok, width = out_grad.shape
    expert = 2 * me + place // (groups // 2)
    corners = [3] if chips == 4 else []
    sides = [j for j in range(1, chips) if j not in corners]
    far_weights, weights3 = (
        [pltpu.with_memory_space_constraint(x[0], space) for x in (w_down, w_gate, w_up)]
        for space in (pltpu.HBM, pltpu.VMEM)
    )

    load, low, high, seg_col, seg_row = make_load(
        parity, out_grad, gate_values.T, expert_ids.T, segment_ids[None, :]
    )

    def whole(x):
        return [(x, q) for q in range(4)]

    near, far = {0: whole(load)}, {}
    corner_half = {j: [swap(x, "ctx", 2 * j) for x in (low, high)] for j in corners}
    far[0] = whole(swap(load, "ctx", 1))
    for j in sides:
        near[j] = whole(swap(load, "ctx", 2 * j))

    scal = jnp.stack([expert] + [me ^ r for r in range(shards)] + [me * 0, me * 0 + 1, parity, 1 - parity])
    straight, turned = shards + 1, shards + 3

    def experts(js, order, tokens):
        loads, sources = [], []
        for j in js:
            loads += [near[j], far[j]]
            sources += [1 + 2 * j, 2 + 2 * j]
        low, high, cot, hidden, token = expert_group(
            scal, sources, order, tokens, loads, gate_pre[0], up_pre[0], weights3 if tokens else far_weights, groups
        )
        cots.append(cot)
        hiddens.append(hidden)
        for i, j in enumerate(js):
            sums[j] = [[y[2 * i], swap(y[2 * i + 1], "ctx", 1)] for y in (low, high)]
        return [token]

    def added(xs):
        return sum(x.astype(F32) for x in xs).astype(BF16)

    sums, cots, hiddens = {}, [], []
    for j in corners:
        first, second = corner_half[j]
        third = swap(first, "ep", 1)
        fourth = swap(second, "ep", 1)
        near[j] = [(x, 0) for x in (first, second, third, fourth)]
        far[j] = [(swap(x, "ctx", 1), 0) for x, _ in near[j]]
    for j in sides:
        far[j] = whole(swap(near[j][0][0], "ctx", 1))
    own = forward_states(seg_col, keys, values)
    fwd_near = near_states(own, chips)
    token = experts([0], straight, [])
    for j in corners:
        token = experts([j], turned, token)
    extra, early = {}, {}
    for i, j in enumerate(sides):
        token = experts([j], straight, token)
        if i == 0:
            for k in corners:
                rows = [added(lax.optimization_barrier((*x, *token))[:2]) for x in sums[k]]
                extra[2] = ([swap(rows[0], "ctx", 2 * 1)], [])
                extra[1] = ([], [swap(rows[1], "ctx", 2 * 2)])
                ready = added(lax.optimization_barrier((*sums[1][0], *rows))[:2])
                early[1] = swap(ready, "ctx", 2)
                token = [*token, *rows, ready]
    loads = [(near if r % 2 == 0 else far)[r // 2][1] for r in range(shards)]
    weights = state_weights(me, [(x, b * (width // 4)) for x, b in loads], tok)

    part = width // (2 * groups)
    totals, spreads, rows = [], [], []
    for c in range(2):
        sends = []
        for j in sides:
            if c == 0 and j in early:
                sends.append(early[j])
            else:
                parts = sums[j][c] + extra.get(j, ([], []))[c]
                row = added(lax.optimization_barrier((*parts, *rows))[: len(parts)])
                sends.append(swap(row, "ctx", 2 * j))
                if c == 0:
                    last = row
        rows = [last]
        total = sums[0][c][0].astype(F32) + sums[0][c][1].astype(F32)
        sends = lax.optimization_barrier((*sends, *totals))[: len(sides)]
        for x in sends:
            total = total + x.astype(F32)
        total = total.astype(BF16)
        totals.append(total)
        pieces = []
        for j in range(1, groups):
            piece = lax.dynamic_slice_in_dim(total, (place ^ j) * part, part, 1)
            pieces.append(swap(piece, "ep", j))
        spreads.append(pieces)
    down_grad = dot(jnp.concatenate(hiddens), jnp.concatenate(cots), (0, 0))

    dq, dk_dv, before = None, [], [totals[1]]
    for c in range(2):
        pieces = lax.optimization_barrier((*spreads[c], *before))[: groups - 1]
        head_cot, own = backward_states(place, seg_col, queries, totals[c], pieces, c, 2)
        if c == 0:
            fwd = all_states(lax.optimization_barrier((*fwd_near, own))[:chips])
        back = all_states(near_states(own, chips))
        dq, dk, dv = inner_grads(
            weights, seg_col, seg_row, queries, keys, values, head_cot, fwd, c, 2, dq
        )
        dk_dv = outer_grads(weights, seg_col, keys, values, dk, dv, back, c, 2, dk_dv)
        before = [own, dk]
    return (dq, *dk_dv, down_grad[None])


def solution(mesh):
    return jax.shard_map(
        local,
        mesh=mesh,
        in_specs=(
            P("ctx", None),
            P("ctx", None),
            P("ctx", None),
            P("ctx"),
            P(("ctx", "ep"), None, None, None),
            P(("ctx", "ep"), None, None, None),
            P(("ctx", "ep"), None, None),
            P(("ctx", "ep"), None, None),
            P(("ctx", "ep"), None, None),
            P("ctx", "ep"),
            P("ctx", "ep"),
            P("ctx", "ep"),
        ),
        out_specs=(P("ctx", "ep"), P("ctx", "ep"), P("ctx", "ep"), P(("ctx", "ep"), None, None)),
        check_vma=False,
    )
```
